128 devices in a mesh: block: 16 (over y, z), subtree: 8 (over x, core).
Axes of the slice: x: 4, y: 4, z: 4, core: 2. Of those that a mesh axis runs over, the one named last changes fastest.
Arguments:
- coords: float32 [10, 98304], P(None, ('block', 'subtree')), may hold values from -6 to 6
- inv_length: float32 [10], replicated, may hold values from 0.15 to 0.6
- nugget: float32 [98304], P(('block', 'subtree')), may hold values from 0.3 to 1
- samples: float32 [64, 98304], P('subtree', 'block'), may hold values from -6 to 6
- block_home: int32 [384], replicated, may hold values from 0 to 383, as said below
- neighbours: int32 [384, 4], P(('block', 'subtree')), may hold values from 0 to 383, as said below
- leaf_order: int32 [384, 256], P(('block', 'subtree')), may hold values from 0 to 255, each once within a row
Outputs:
- whitened: float32 [64, 98304], P('subtree', 'block')
- precision_product: float32 [64, 98304], P('subtree', 'block')
The draws below stay inside these ranges and needn't reach their ends.
Inputs may be any that keep to these rules, and one draw needn't show every extreme that they name: `block_home`: A permutation of the 384 block ids: every storage block is the home of exactly one id. Storage block s lies on the device with block index s // (3 * n) and subtree index (s // 3) % n, n the size of the subtree axis. `neighbours`: the 4 ids of a row are distinct and none has the row's own storage block as home; every home lies on a device with the same subtree index as the row's device and a block index at most one away from it.
All inputs are finite; a program needn't handle non-finite values.
Results may differ from the reference program's by a relative error of at most 0.00027.
Values sent between devices are 32-bit elements; how exact they have to be, the bound alone decides.
No kernel may reach another device: no remote copies, remote signals or barrier semaphores. Data moves between devices by JAX's collectives and lax.ppermute only.
A program may use at most 128 MiB of HBM per device.

```python
import math
import jax
import jax.numpy as jnp
from jax import lax

DIMS = 10
BS = 256
NNB = 4
NVEC = 64
BLK_DEV = 3
NBLK = 384
NPTS = 98304
N_BLOCK = 16
N_SUBTREE = 8


def neighbour_tables(key):
    home_key = jax.random.fold_in(key, 101)
    score_key = jax.random.fold_in(key, 202)
    block_home = jax.random.permutation(home_key, NBLK).astype(jnp.int32)
    label_of = jnp.zeros((NBLK,), jnp.int32).at[block_home].set(jnp.arange(NBLK, dtype=jnp.int32))
    storage = jnp.arange(NBLK, dtype=jnp.int32)
    device = storage // BLK_DEV
    tree_row = device // N_SUBTREE
    column = device % N_SUBTREE
    offsets = jnp.arange(3 * BLK_DEV, dtype=jnp.int32)
    near_row = tree_row[:, None] + offsets[None, :] // BLK_DEV - 1
    candidate = (near_row * N_SUBTREE + column[:, None]) * BLK_DEV + offsets[None, :] % BLK_DEV
    usable = (near_row >= 0) & (near_row < N_BLOCK) & (candidate != storage[:, None])
    scores = jax.random.randint(score_key, (NBLK, 3 * BLK_DEV), 0, 1 << 20, dtype=jnp.int32) * (3 * BLK_DEV) + offsets[None, :]
    scores = jnp.where(usable, scores, -1)
    picked = lax.top_k(scores, NNB)[1]
    chosen = jnp.clip(jnp.take_along_axis(candidate, picked, axis=1), 0, NBLK - 1)
    return (block_home, label_of[chosen])


def draw_block_home(key, part):
    return neighbour_tables(key)[0]


def draw_neighbours(key, part):
    return neighbour_tables(key)[1]


def level_of(key, extent, split, least, high):
    loudness, own = 1.0, jax.random.fold_in(key, 6)
    for dim, blocks in split:
        heights = jnp.exp(jax.random.uniform(jax.random.fold_in(own, dim), (blocks,), jnp.float32, least / len(split), high / len(split)))
        loudness = loudness * jnp.repeat(heights, extent[dim] // blocks).reshape([-1 if axis == dim else 1 for axis in range(len(extent))])
    return loudness


def scatter_about(own_key, shape, deviation, limit, shards=(), held_as=jnp.bfloat16):
    loudness = level_of(own_key, shape, shards, -0.22, 0.18) if shards else 1.0
    values = jax.random.normal(own_key, shape, jnp.float32) * deviation * loudness
    return jnp.minimum(jnp.maximum(values, -limit), limit).astype(held_as)


def setup_inputs(seed: int = 0) -> dict:
    key_list = jax.random.split(jax.random.key(seed), 8)
    return {
        "coords": scatter_about(key_list[0], (DIMS, NPTS), 1.0, 6.0, ((1, 128),), jnp.float32),
        "inv_length": jnp.clip(jnp.exp(jax.random.uniform(key_list[1], (DIMS,), jnp.float32, math.log(0.15), math.log(0.6))), 0.15, 0.6),
        "nugget": jnp.clip(0.3 + 0.7 * jax.random.uniform(key_list[2], (NPTS,), jnp.float32) ** level_of(key_list[2], (NPTS,), ((0, 128),), -0.2, 0.2), 0.3, 1.0),
        "samples": scatter_about(key_list[3], (NVEC, NPTS), 1.0, 6.0, ((0, 8), (1, 16)), jnp.float32),
        "block_home": draw_block_home(jax.random.fold_in(key_list[7], 71), 0),
        "neighbours": draw_neighbours(jax.random.fold_in(key_list[7], 71), 0),
        "leaf_order": jax.vmap(lambda own: jax.random.permutation(own, BS))(jax.random.split(key_list[6], NBLK)).reshape((NBLK, BS)).astype(jnp.int32),
    }


SQRT_THREE = math.sqrt(3.0)

def matern(left, right, inv_length):
    summed = jnp.zeros((left.shape[1], right.shape[1]), jnp.float32)
    for coord_index in range(left.shape[0]):
        gap = (left[coord_index][:, None] - right[coord_index][None, :]) * inv_length[coord_index]
        summed = summed + gap * gap
    scaled = SQRT_THREE * jnp.sqrt(summed)
    return (1.0 + scaled) * jnp.exp(-scaled)

def factor_block(near_coords, near_nugget, own_coords, own_nugget, inv_length):
    k_near = matern(near_coords, near_coords, inv_length) + jnp.diag(near_nugget)
    k_cross = matern(near_coords, own_coords, inv_length)
    k_own = matern(own_coords, own_coords, inv_length) + jnp.diag(own_nugget)
    near_chol = jnp.linalg.cholesky(k_near)
    cross_solve = lax.linalg.triangular_solve(near_chol, k_cross, left_side=True, lower=True)
    schur = k_own - jnp.dot(cross_solve.T, cross_solve, precision=lax.Precision.HIGHEST)
    own_chol = jnp.linalg.cholesky(schur)
    return (near_chol, cross_solve, own_chol)

def apply_block(near_chol, cross_solve, own_chol, near_samples, own_samples):
    near_white = lax.linalg.triangular_solve(near_chol, near_samples, left_side=False, lower=True, transpose_a=True)
    predicted = jnp.dot(near_white, cross_solve, precision=lax.Precision.HIGHEST)
    whiten = lax.linalg.triangular_solve(own_chol, own_samples - predicted, left_side=False, lower=True, transpose_a=True)
    back_term = lax.linalg.triangular_solve(own_chol, whiten, left_side=False, lower=True, transpose_a=False)
    spread = jnp.dot(back_term, cross_solve.T, precision=lax.Precision.HIGHEST)
    near_term = -lax.linalg.triangular_solve(near_chol, spread, left_side=False, lower=True, transpose_a=False)
    return (whiten, back_term, near_term)

def reference(coords, inv_length, nugget, samples, block_home, neighbours, leaf_order):
    block_count = neighbours.shape[0]
    near_count = neighbours.shape[1]
    leaf_size = leaf_order.shape[1]
    coord_count = coords.shape[0]
    vectors = samples.shape[0]
    coord_blocks = coords.reshape(coord_count, block_count, leaf_size)
    nugget_blocks = nugget.reshape(block_count, leaf_size)
    sample_blocks = samples.reshape(vectors, block_count, leaf_size)

    def one_block(storage):
        home_ids = block_home[neighbours[storage]]
        leaf_perm = leaf_order[storage]
        near_coords = coord_blocks[:, home_ids, :].reshape(coord_count, near_count * leaf_size)
        near_nugget = nugget_blocks[home_ids].reshape(near_count * leaf_size)
        near_samples = sample_blocks[:, home_ids, :].reshape(vectors, near_count * leaf_size)
        own_coords = jnp.take(coord_blocks[:, storage, :], leaf_perm, axis=1)
        own_nugget = jnp.take(nugget_blocks[storage], leaf_perm)
        own_samples = jnp.take(sample_blocks[:, storage, :], leaf_perm, axis=1)
        near_chol, cross_solve, own_chol = factor_block(near_coords, near_nugget, own_coords, own_nugget, inv_length)
        whiten, back_term, near_term = apply_block(near_chol, cross_solve, own_chol, near_samples, own_samples)
        own_term = jnp.zeros_like(back_term).at[:, leaf_perm].set(back_term)
        return (whiten, own_term, near_term.reshape(vectors, near_count, leaf_size), home_ids)
    whiten_all, own_all, near_all, homes_all = lax.map(one_block, jnp.arange(block_count, dtype=jnp.int32))
    whitened = whiten_all.transpose(1, 0, 2).reshape(vectors, block_count * leaf_size)
    spread = near_all.transpose(0, 2, 1, 3).reshape(block_count * near_count, vectors, leaf_size)
    summed = own_all.at[homes_all.reshape(block_count * near_count)].add(spread)
    precision_product = summed.transpose(1, 0, 2).reshape(vectors, block_count * leaf_size)
    return (whitened, precision_product)
```

```python
import functools
import math

import jax
import jax.numpy as jnp
from jax import lax
from jax.experimental import pallas as pl
from jax.experimental.pallas import tpu as pltpu
from jax.sharding import PartitionSpec as P

F32 = jnp.float32
BF16 = jnp.bfloat16
SQRT_THREE = math.sqrt(3.0)
LEAST_EIGENVALUE = 0.29
NEWTON_END = 1e-5
PRECISE_NORM = 24.0
ROWS = 16
FEATURES = 128
FINE_STEPS = 2
BESIDE = 2
NN = ((1,), (0,))
NT = ((1,), (1,))


def newton_limits():
    ratio, limits = 1.0 - NEWTON_END, []
    while LEAST_EIGENVALUE / ratio < 600.0:
        root = math.sqrt(1.0 - ratio)
        ratio = (1.0 - root) / (1.0 + root)
        limits.append(LEAST_EIGENVALUE / ratio)
    return limits


def split(x):
    high = x.astype(BF16)
    return high, (x - high.astype(F32)).astype(BF16)


def split3(x):
    high = x.astype(BF16)
    rest = x - high.astype(F32)
    middle = rest.astype(BF16)
    return high, middle, (rest - middle.astype(F32)).astype(BF16)


def left(high, low):
    return jnp.concatenate([high, high, low], axis=1)


def right_rows(high, low):
    return jnp.concatenate([high, low, high], axis=0)


def right_cols(high, low):
    return jnp.concatenate([high, low, high], axis=1)


def left6(high, middle, low):
    return jnp.concatenate([high, high, middle, high, low, middle], axis=1)


def right6(high, middle, low):
    return jnp.concatenate([high, middle, high, low, high, middle], axis=0)


def precise_product(a, b):
    return mm(left6(*split3(a)), right6(*split3(b)), NN)


def mm(a, b, dims):
    return lax.dot_general(a, b, (dims, ((), ())), preferred_element_type=F32)


def eye_mask(n):
    return lax.broadcasted_iota(jnp.int32, (n, n), 0) == lax.broadcasted_iota(jnp.int32, (n, n), 1)


def halves_of(both):
    width = both.shape[-1] // 2
    return both[..., :width], both[..., width:]


def permutation(leaf_row):
    n = leaf_row.shape[1]
    rows = lax.broadcasted_iota(jnp.int32, (n, n), 0)
    return jnp.where(rows == leaf_row, 1.0, 0.0).astype(BF16)


def off_diagonal(x, eye):
    diagonal = jnp.sum(jnp.where(eye, x, 0.0), axis=0, keepdims=True)
    return diagonal, split(jnp.where(eye, 0.0, x))


def scaled_product(mat, mat_split, diagonal, rest):
    return mat * diagonal + mm(left(*mat_split), right_rows(*rest), NN)


def stacked_product(x, high, low, dims):
    n = x.shape[0]
    x_high, x_low = split(x)
    both = mm(jnp.concatenate([x_high, x_low], axis=0), high, dims)
    return both[:n] + (both[n:] + mm(x_high, low, dims))


def newton_inverse(mat_at, count, mats, a_left, x_ref, limits, beside=None):
    n = x_ref.shape[1]
    eye = eye_mask(n)
    norm = None
    for q in range(count):
        mat = mat_at(q)
        mats[q] = mat
        a_left[q] = jnp.concatenate(split(mat), axis=1)
        sums = jnp.sum(jnp.abs(mat), axis=0, keepdims=True)
        norm = sums if norm is None else jnp.maximum(norm, sums)
    bound = jnp.max(norm, axis=1, keepdims=True)
    trips = jnp.int32(0)
    bound_scalar = jnp.max(norm)
    for limit in limits:
        trips += (bound_scalar > limit).astype(jnp.int32)
    scale0 = 1.0 / bound
    gap = 1.0 - LEAST_EIGENVALUE * scale0
    first = scale0 * (2.0 / (2.0 - gap))
    for q in range(count):
        x_ref[q] = jnp.where(eye, 2.0 * first, 0.0) - (first * first) * mats[q]
    ratio = gap / (2.0 - gap)

    def rough_body(trip, gap):
        step = 2.0 / (2.0 - gap)
        for q in range(count):
            x = x_ref[q]
            diagonal, _ = off_diagonal(x, eye)
            rest = jnp.where(eye, 0.0, x).astype(BF16)
            product = mats[q] * diagonal + mm(a_left[q][:, :n], rest, NN)
            r = jnp.where(eye, 1.0, 0.0) - product
            x_ref[q] = step * (2.0 - step) * x + (step * step) * mm(x.astype(BF16), r.astype(BF16), NN)
        ratio = gap / (2.0 - gap)
        return ratio * ratio

    def body(trip, gap):
        step = 2.0 / (2.0 - gap)
        for q in range(count):
            x = x_ref[q]
            diagonal, rest = off_diagonal(x, eye)
            product = scaled_product(mats[q], halves_of(a_left[q]), diagonal, rest)
            r = jnp.where(eye, 1.0, 0.0) - product
            change = mm(left(*split(x)), right_rows(*split(r)), NN)
            x_ref[q] = step * (2.0 - step) * x + (step * step) * change
            if beside is not None:
                beside(trip, q)
        ratio = gap / (2.0 - gap)
        return ratio * ratio

    precise = bound_scalar > PRECISE_NORM
    trips = trips - precise.astype(jnp.int32)
    rough = jnp.where(precise, 0, jnp.maximum(trips - FINE_STEPS, 0)) if beside is None else 0
    gap = lax.fori_loop(0, rough, rough_body, ratio * ratio) if beside is None else ratio * ratio
    lax.fori_loop(rough, trips, body, gap)

    @pl.when(precise)
    def _():
        for q in range(count):
            x = x_ref[q]
            r = jnp.where(eye, 1.0, 0.0) - precise_product(mats[q], x)
            x_ref[q] = x + mm(left(*split(x)), right_rows(*split(r)), NN)

    return trips, precise


def tile_index(i, k):
    return i * (i + 1) // 2 + k


def link_index(i, j):
    return i * (i - 1) // 2 + j


def factor_kernel(
    picks, inv_length, low_ref, mid_ref, high_ref, leaf_ref,
    t_out, oi_ref,
    ext, feat_l, feat_r, nug, a, a_split, t_split, mats, a_left, x_ref, x_rest, x_diagonal,
    half_mats, half_left, half_x, sent,
):
    blocks, near = picks.shape
    dims = inv_length.shape[0]
    tile = leaf_ref.shape[1]
    half, quarter = tile // 2, tile // 4
    each = range(blocks)

    for part, source in enumerate((low_ref, mid_ref, high_ref)):
        start = source.shape[1] - 2 * blocks * tile
        for b in each:
            first, second = start + b * tile, start + (blocks + b) * tile
            ext[part * blocks + b] = jnp.concatenate(
                [source[:, first : first + tile], source[:, second : second + tile]], axis=0
            )

    row_id = lax.broadcasted_iota(jnp.int32, (ROWS, tile), 0)
    scale = jnp.zeros((ROWS, tile), F32)
    for d in range(dims):
        scale = jnp.where(row_id == d, inv_length[d] * SQRT_THREE, scale)

    def features(g):
        c = g * scale
        h, m, l = split3(c)
        nh, nm, nl = split3(jnp.sum(c * c, axis=0, keepdims=True))
        nh, nm, nl = nh.astype(F32), nm.astype(F32), nl.astype(F32)
        norm_first = jnp.where(row_id == 0, nh, jnp.where(row_id == 1, nm, jnp.where(row_id == 2, nl, 0.0)))
        norm_last = jnp.where(row_id == 3, nh, jnp.where(row_id == 4, nm, jnp.where(row_id == 5, nl, 0.0)))
        norm_l = jnp.where((row_id >= 3) & (row_id < 6), 1.0, norm_first).astype(BF16)
        norm_r = jnp.where(row_id < 3, 1.0, norm_last).astype(BF16)
        zero = jnp.zeros((ROWS, tile), BF16)
        lhs = jnp.concatenate([h, h, m, h, l, m, norm_l, zero], axis=0)
        two_h, two_m, two_l = ((-2.0 * part.astype(F32)).astype(BF16) for part in (h, m, l))
        rhs = jnp.concatenate([two_h, two_m, two_h, two_l, two_h, two_m, norm_r, zero], axis=0)
        return lhs, rhs

    for s in each:
        for n in range(near):
            g = ext[picks[s, n]]
            lhs, rhs = features(g)
            feat_l[s, n] = lhs.astype(F32).T.astype(BF16)
            feat_r[s, n] = rhs
            nug[s, n] = jnp.broadcast_to(g[dims : dims + 1, :], (8, tile))
        g = ext[blocks + s]
        perm = permutation(leaf_ref[s : s + 1, :])
        h, m, l = split3(g)
        g = mm(jnp.concatenate([h, m, l], axis=1), jnp.concatenate([perm] * 3, axis=0), NN)
        lhs, rhs = features(g)
        feat_l[s, near] = lhs.astype(F32).T.astype(BF16)
        feat_r[s, near] = rhs
        nug[s, near] = jnp.broadcast_to(g[dims : dims + 1, :], (8, tile))

    def matern(s, i, k):
        d = jnp.maximum(mm(feat_l[s, i], feat_r[s, k], NN), 0.0)
        r = d * lax.rsqrt(d + 1e-30)
        return (1.0 + r) * jnp.exp(-r)

    eye = eye_mask(tile)

    total = tile_index(near + 1, 0)

    def build(at, which):
        i = sum(((at >= tile_index(row, 0)).astype(jnp.int32) for row in range(1, near + 1)), jnp.int32(0))
        k = at - tile_index(i, 0)
        mask = eye & (i == k)
        for s in which:
            a[s, at] = jnp.where(mask, 1.0 + nug[s, i][0:1, :], matern(s, i, k))

    for s in each:
        a[s, 0] = jnp.where(eye, 1.0 + nug[s, 0][0:1, :], matern(s, 0, 0))

    def build_beside(trip, s):
        for u in range(BESIDE):
            build(jnp.minimum(1 + BESIDE * trip + u, total - 1), (s,))

    def build_rest(at, carry):
        build(at, each)
        return carry

    limits = newton_limits()

    def finish_panel(j, precise):
        for s in each:
            x_diagonal[s], rest = off_diagonal(x_ref[s], eye)
            x_rest[s] = jnp.concatenate(rest, axis=1)

        def scale_row(i, inner):
            for s in each:
                at = tile_index(i, j)
                mat = a[s, at]
                parts = split(mat)
                a_split[s, i] = jnp.concatenate(parts, axis=1)
                t = scaled_product(mat, parts, x_diagonal[s], halves_of(x_rest[s]))
                t_split[s, link_index(i, j)] = jnp.concatenate(split(t), axis=1)
            return inner

        def scale_row_precisely(i, inner):
            for s in each:
                at = tile_index(i, j)
                mat = a[s, at]
                a_split[s, i] = jnp.concatenate(split(mat), axis=1)
                t_split[s, link_index(i, j)] = jnp.concatenate(split(precise_product(mat, x_ref[s])), axis=1)
            return inner

        @pl.when(precise)
        def _():
            lax.fori_loop(j + 1, near + 1, scale_row_precisely, 0)

        @pl.when(jnp.logical_not(precise))
        def _():
            lax.fori_loop(j + 1, near + 1, scale_row, 0)

        def update_row(i, inner):
            def update(k, innermost):
                for s in each:
                    t = left(*halves_of(t_split[s, link_index(i, j)]))
                    at = tile_index(i, k)
                    a[s, at] -= mm(t, right_cols(*halves_of(a_split[s, k])), NT)
                return innermost

            lax.fori_loop(j + 1, i + 1, update, 0)
            return inner

        lax.fori_loop(j + 1, near + 1, update_row, 0)

    trips, precise = newton_inverse(lambda s: a[s, 0], blocks, mats, a_left, x_ref, limits, build_beside)
    lax.fori_loop(jnp.minimum(1 + BESIDE * trips, total), total, build_rest, 0)
    finish_panel(0, precise)

    def panel(j, carry):
        _, precise = newton_inverse(lambda s: a[s, tile_index(j, j)], blocks, mats, a_left, x_ref, limits)
        finish_panel(j, precise)
        return carry

    lax.fori_loop(1, near, panel, 0)
    sending = pltpu.make_async_copy(t_split, t_out, sent)
    sending.start()

    own = total - 1
    newton_inverse(lambda s: a[s, own, :half, :half], blocks, half_mats, half_left, half_x, limits)
    links, quads = [], []
    for s in each:
        a21 = a[s, own, half:, :half]
        parts = split(a21)
        b = precise_product(a21, half_x[s])
        links.append(b)
        quads.append((a[s, own, :half, :half], a[s, own, half:, half:] - mm(left(*split(b)), right_cols(*parts), NT)))

    lanes_q = lax.broadcasted_iota(jnp.int32, (quarter, half), 1)
    first_half = lanes_q < quarter

    def on_diagonal(upper, lower):
        return jnp.concatenate(
            [jnp.where(first_half, upper, 0.0), jnp.where(first_half, 0.0, lower)], axis=0
        )

    def swap(x):
        return pltpu.roll(x, quarter, 1)

    heads, unders, tails = [], [], []
    for q0, q1 in quads:
        heads.append(on_diagonal(q0[:quarter], swap(q1[:quarter])))
        unders.append(on_diagonal(q0[quarter:], swap(q1[quarter:])))
        tails.append(on_diagonal(swap(q0[quarter:]), q1[quarter:]))
    newton_inverse(lambda s: heads[s], blocks, half_mats, half_left, half_x, limits)
    joins, packed, scales = [], [], []
    for s in each:
        under = split(unders[s])
        b = precise_product(unders[s], half_x[s])
        joins.append(b)
        for m in (heads[s], tails[s] - mm(left(*split(b)), right_cols(*under), NT)):
            m = jnp.where(first_half, m[:quarter], m[quarter:])
            packed.append([m[r : r + 8] for r in range(0, quarter, 8)])
            scales.append([None] * (quarter // 8))

    rows_8 = lax.broadcasted_iota(jnp.int32, (8, half), 0)
    lanes_8 = lax.broadcasted_iota(jnp.int32, (8, half), 1)
    column = lanes_8 % quarter
    for t in range(quarter):
        pick = lanes_8 - column + t
        group, row = divmod(t, 8)
        for q, parts in enumerate(packed):
            factor = jnp.take_along_axis(parts[group], pick, axis=1)
            pivot = factor[row : row + 1, :]
            line = parts[group][row : row + 1, :]
            line = jnp.where(column[0:1, :] == t, line + 1.0, line) * (1.0 / pivot)
            root = lax.rsqrt(pivot)
            scales[q][group] = jnp.where(rows_8 == row, root, 0.0 if row == 0 else scales[q][group])
            parts[group] = parts[group] - jnp.where(rows_8 > row, factor, 0.0) * line
            for r in range(group + 1, quarter // 8):
                parts[r] = parts[r] - jnp.take_along_axis(parts[r], pick, axis=1) * line

    rows_q = lax.broadcasted_iota(jnp.int32, (quarter, half), 0)
    column_q = lanes_q % quarter
    for s in each:
        inverses = []
        for q in (2 * s, 2 * s + 1):
            unit = jnp.where(column_q == rows_q, 1.0, 0.0)
            m = jnp.where(column_q < rows_q, jnp.concatenate(packed[q], axis=0), unit)
            m = m * jnp.concatenate(scales[q], axis=0)
            inverses.append(on_diagonal(m, m))
        head, tail = inverses
        join = -mm(left(*split(tail)), right_rows(*split(joins[s])), NN)
        zero = jnp.zeros((quarter, half), F32)
        h0 = jnp.concatenate(
            [jnp.where(first_half, head[:quarter], 0.0), jnp.where(first_half, join[:quarter], swap(tail[:quarter]))],
            axis=0,
        )
        h1 = jnp.concatenate(
            [swap(head[quarter:]), jnp.where(first_half, swap(join[quarter:]), tail[quarter:])], axis=0
        )
        corner = -mm(left(*split(h1)), right_rows(*split(links[s])), NN)
        inverse = jnp.concatenate(
            [
                jnp.concatenate([h0, jnp.zeros((half, half), F32)], axis=1),
                jnp.concatenate([corner, h1], axis=1),
            ],
            axis=0,
        )
        oi_ref[s] = inverse
    sending.wait()


def factor_blocks(picks, inv_length, extended, leaf):
    blocks, near = picks.shape
    tile = leaf.shape[1]
    tiles, links = tile_index(near + 1, 0), link_index(near + 1, 0)
    half = tile // 2
    vmem = pl.BlockSpec(memory_space=pltpu.VMEM)
    smem = pl.BlockSpec(memory_space=pltpu.SMEM)
    return pl.pallas_call(
        factor_kernel,
        out_shape=(
            jax.ShapeDtypeStruct((blocks, links, tile, 2 * tile), BF16),
            jax.ShapeDtypeStruct((blocks, tile, tile), F32),
        ),
        in_specs=[smem] * 2 + [vmem] * 4,
        out_specs=(pl.BlockSpec(memory_space=pl.ANY), vmem),
        scratch_shapes=[
            pltpu.VMEM((3 * blocks, ROWS, tile), F32),
            pltpu.VMEM((blocks, near + 1, tile, FEATURES), BF16),
            pltpu.VMEM((blocks, near + 1, FEATURES, tile), BF16),
            pltpu.VMEM((blocks, near + 1, 8, tile), F32),
            pltpu.VMEM((blocks, tiles, tile, tile), F32),
            pltpu.VMEM((blocks, near + 1, tile, 2 * tile), BF16),
            pltpu.VMEM((blocks, links, tile, 2 * tile), BF16),
            pltpu.VMEM((blocks, tile, tile), F32),
            pltpu.VMEM((blocks, tile, 2 * tile), BF16),
            pltpu.VMEM((blocks, tile, tile), F32),
            pltpu.VMEM((blocks, tile, 2 * tile), BF16),
            pltpu.VMEM((blocks, 1, tile), F32),
            pltpu.VMEM((blocks, half, half), F32),
            pltpu.VMEM((blocks, half, 2 * half), BF16),
            pltpu.VMEM((blocks, half, half), F32),
            pltpu.SemaphoreType.DMA,
        ],
        name="factor",
    )(picks, inv_length, *extended, leaf)


def apply_kernel(
    picks, samples_ref, leaf_ref, t_in, oi_ref,
    white_ref, out_low, out_mid, out_high,
    ext, acc, links, received,
):
    blocks, near = picks.shape
    tile = leaf_ref.shape[1]
    each = range(blocks)
    order = [(i, j) for j in range(near) for i in range(j + 1, near + 1)]
    arrivals = {}
    for i, j in order:
        at = link_index(i, j)
        arrivals[i, j] = pltpu.make_async_copy(t_in.at[:, at], links.at[at], received.at[at])
        arrivals[i, j].start()
    for b in range(3 * blocks):
        ext[b] = samples_ref[:, b * tile : (b + 1) * tile]
    acc[...] = jnp.zeros_like(acc)
    owns, perms = [], []
    for s in each:
        perm = permutation(leaf_ref[s : s + 1, :])
        own = mm(jnp.concatenate(split3(ext[blocks + s]), axis=1), jnp.concatenate([perm] * 3, axis=0), NN)
        perms.append(perm)
        owns.append(own)
    parts = [[ext[picks[s, n]] for n in range(near)] + [owns[s]] for s in each]
    for j in range(near):
        for i in range(j + 1, near + 1):
            arrivals[i, j].wait()
        for i in range(j + 1, near + 1):
            for s in each:
                parts[s][i] -= stacked_product(parts[s][j], *halves_of(links[link_index(i, j), s]), NT)
    inverses = [split(oi_ref[s]) for s in each]
    whites = [stacked_product(parts[s][near], *inverses[s], NT) for s in each]
    backs = [stacked_product(whites[s], *inverses[s], NN) for s in each]
    for s in each:
        white_ref[:, s * tile : (s + 1) * tile] = whites[s]
        acc[blocks + s] = mm(
            jnp.concatenate(split3(backs[s]), axis=1), jnp.concatenate([perms[s]] * 3, axis=1), NT
        )
    terms = [
        [-stacked_product(backs[s], *halves_of(links[link_index(near, j), s]), NN) for j in range(near)] for s in each
    ]
    for i in range(near - 1, -1, -1):
        for j in range(i):
            for s in each:
                terms[s][j] -= stacked_product(terms[s][i], *halves_of(links[link_index(i, j), s]), NN)
    for s in each:
        for i in range(near):
            acc[picks[s, i]] += terms[s][i]
    for part, out in enumerate((out_low, out_mid, out_high)):
        for b in each:
            out[:, b * tile : (b + 1) * tile] = acc[part * blocks + b]


def apply_blocks(picks, samples, leaf, t, oi):
    blocks = picks.shape[0]
    tile = leaf.shape[1]
    vectors = samples.shape[0]
    vmem = pl.BlockSpec(memory_space=pltpu.VMEM)
    out = jax.ShapeDtypeStruct((vectors, blocks * tile), F32)
    return pl.pallas_call(
        apply_kernel,
        out_shape=(out,) * 4,
        in_specs=[pl.BlockSpec(memory_space=pltpu.SMEM), vmem, vmem, pl.BlockSpec(memory_space=pl.ANY), vmem],
        out_specs=(vmem,) * 4,
        scratch_shapes=[
            pltpu.VMEM((3 * blocks, vectors, tile), F32),
            pltpu.VMEM((3 * blocks, vectors, tile), F32),
            pltpu.VMEM((t.shape[1], blocks) + t.shape[2:], BF16),
            pltpu.SemaphoreType.DMA((t.shape[1],)),
        ],
        name="apply",
    )(picks, samples, leaf, t, oi)


def shifted(block, axis, distance):
    count = lax.axis_size(axis)
    route = [(i - distance, i) for i in range(count) if 0 <= i - distance < count]
    return lax.ppermute(block, axis, route)


def per_device(coords, inv_length, nugget, samples, block_home, neighbours, leaf_order):
    subtrees = lax.axis_size("subtree")
    tree_row = lax.axis_index("block")
    local_blocks = neighbours.shape[0]
    span_width = coords.shape[1]

    geometry = jnp.concatenate(
        [coords, nugget.reshape(1, span_width), jnp.zeros((ROWS - 1 - coords.shape[0], span_width), F32)], axis=0
    )
    packed = jnp.concatenate([samples, geometry[: ROWS // 2], geometry[ROWS // 2 :]], axis=1)
    extended = (shifted(packed, "block", 1), packed, shifted(packed, "block", -1))
    columns = jnp.stack([source[:, : samples.shape[1]] for source in extended])
    columns = columns.reshape(3, samples.shape[0], subtrees, span_width).transpose(1, 2, 0, 3)
    columns = columns.reshape(samples.shape[0], 3 * samples.shape[1])
    block_samples = lax.all_to_all(columns, "subtree", split_axis=1, concat_axis=0, tiled=True)

    all_ids = jnp.arange(block_home.shape[0], dtype=jnp.int32)
    home_ids = jnp.sum(jnp.where(neighbours[:, :, None] == all_ids, block_home, 0), axis=2)
    home_device = home_ids // local_blocks
    picks = (home_device // subtrees - tree_row + 1) * local_blocks + home_ids % local_blocks

    t, oi = factor_blocks(picks, inv_length, extended, leaf_order)
    white, lower, middle, upper = apply_blocks(picks, block_samples, leaf_order, t, oi)
    summed = middle + shifted(lower, "block", -1) + shifted(upper, "block", 1)
    both = lax.all_to_all(jnp.stack([white, summed]), "subtree", split_axis=1, concat_axis=2, tiled=True)
    return both[0], both[1]


def solution(mesh):
    return jax.shard_map(
        per_device,
        mesh=mesh,
        in_specs=(
            P(None, ("block", "subtree")),
            P(),
            P(("block", "subtree")),
            P("subtree", "block"),
            P(),
            P(("block", "subtree"), None),
            P(("block", "subtree"), None),
        ),
        out_specs=(P("subtree", "block"), P("subtree", "block")),
        check_vma=False,
    )
```
